128 devices in a mesh: req: 16 (over y, x_hi, core), tp: 8 (over x_lo, z).
Axes of the slice: x: 4 (x_hi: 2, x_lo: 2; x = x_hi * 2 + x_lo), y: 4, z: 4, core: 2. Of those that a mesh axis runs over, the one named last changes fastest.
Arguments:
- hidden_in: bfloat16 [16384, 7168], P(('req', 'tp')), may hold values from -6 to 6
- ln_gain: float32 [7168], replicated, may hold values from 0.1 to 1.9
- ln_bias: float32 [7168], replicated, may hold values from -3 to 3
- w_query: bfloat16 [7168, 4096], P(None, 'tp'), may hold values from -0.0625 to 0.0625
- w_key: bfloat16 [7168, 4096], P(None, 'tp'), may hold values from -0.0625 to 0.0625
- w_value: bfloat16 [7168, 4096], P(None, 'tp'), may hold values from -0.0625 to 0.0625
- qkv_bias: float32 [3, 4096], P(None, 'tp'), may hold values from -34 to 34
- segment_ids: int32 [16384], P('req'), may hold values from -1 to 19, as said below
- page_table: int32 [1024], P('req'), may hold values from 0 to 1023, as said below
Outputs:
- context: bfloat16 [16384, 4096], P('req', 'tp')
- kv_cache: bfloat16 [2, 32, 1024, 16, 128], P(None, 'tp', 'req')
The draws below stay inside these ranges and needn't reach their ends.
Inputs may be any that keep to these rules, and one draw needn't show every extreme that they name: `segment_ids`: within each block of 1024 positions, live positions come first and padding (-1) fills the tail; ids count the block's requests from 0 upward, each request contiguous and starting at a multiple of 32 positions within its block. In every draw one block holds a single request of exactly 1024 positions; every other request has at most 256 positions. `page_table`: every slot is named once. Of the 64 pages of one block of 1024 positions, exactly 4 name slots s with s // 64 equal to each given value.
All inputs are finite; a program needn't handle non-finite values.
Results may differ from the reference program's by a relative error of at most 0.012.
The reference program's roundings to bfloat16 on the way (of `normed`, `query` and `probs`) count: a program that leaves them out, or rounds other values in their place, can miss the bound.
Values may be sent and summed in bfloat16 or wider, within the bound.
A program may use at most 128 MiB of HBM per device.

```python
import jax
import jax.numpy as jnp
from jax import lax

D = 7168
HEADS = 32
HEAD_DIM = 128
CAP = 1024
PAGE = 16
PAGES_DEV = 64
ROWS = 16384
SLOTS = 1024
N_REQ = 16


def draw_qkv_bias(key, part):
    keys = jax.random.split(key, 8)
    width = HEADS * HEAD_DIM
    base = 0.5 * jnp.clip(jax.random.normal(keys[0], (3, width), jnp.float32), -6.0, 6.0)
    low_strength = 120.0
    high_strength = 260.0
    signs = (jax.random.randint(keys[1], (HEADS, HEAD_DIM), 0, 2) * 2 - 1).astype(jnp.float32)
    key_size = jax.random.uniform(keys[2], (HEADS, HEAD_DIM), jnp.float32, 2.0, 3.5)
    query_size = jax.random.uniform(keys[3], (HEADS, HEAD_DIM), jnp.float32, 0.7, 1.3)
    heads = jnp.arange(HEADS)
    strong = jax.random.randint(keys[4], (), 0, HEADS)
    weak = (strong + 1 + jax.random.randint(keys[5], (), 0, HEADS - 1)) % HEADS
    aligned = jax.random.randint(keys[6], (HEADS,), 0, 2) == 1
    aligned = (aligned | (heads == strong)) & (heads != weak)
    target = jax.random.uniform(keys[7], (HEADS,), jnp.float32, low_strength, high_strength)
    target = jnp.where(heads == strong, high_strength, target)
    factor = target / (2.75 * HEAD_DIM ** 0.5)
    query_bias = signs * query_size * factor[:, None]
    key_bias = signs * key_size
    query_row = jnp.where(aligned[:, None], query_bias, base[0].reshape(HEADS, HEAD_DIM)).reshape(-1)
    key_row = jnp.where(aligned[:, None], key_bias, base[1].reshape(HEADS, HEAD_DIM)).reshape(-1)
    return jnp.stack([query_row, key_row, base[2]]).astype(jnp.float32)


def draw_segment_ids(key, part):
    key_long, key_fill, key_cuts, key_dense = jax.random.split(key, 4)
    long_group = jax.random.randint(key_long, (), 0, N_REQ)
    dense_group = (long_group + 1 + jax.random.randint(key_dense, (), 0, N_REQ - 1)) % N_REQ
    groups = jnp.arange(N_REQ)
    fill = jax.random.randint(key_fill, (N_REQ,), CAP // 8, 5 * CAP // 8 + 1)
    fill = jnp.where(groups == dense_group, 5 * CAP // 8, fill)
    fill = jnp.where(groups == long_group, CAP, fill)
    position = jnp.arange(CAP)
    unit_cuts = jax.random.randint(key_cuts, (N_REQ, CAP // 32), 0, 2) == 0
    cuts = jnp.repeat(unit_cuts, 32, axis=1) & (position % 32 == 0)[None, :]
    cuts = jnp.where((groups == dense_group)[:, None], (position % 32 == 0)[None, :], cuts)
    starts = cuts | (position % 256 == 0)[None, :]
    starts = jnp.where((groups == long_group)[:, None], (position == 0)[None, :], starts)
    ids = jnp.cumsum(starts.astype(jnp.int32), axis=1) - 1
    ids = jnp.where(position[None, :] < fill[:, None], ids, -1)
    return ids.reshape(-1).astype(jnp.int32)


def draw_page_table(key, part):
    key_send, key_place = jax.random.split(key, 2)
    share = PAGES_DEV // N_REQ
    sends = jax.vmap(lambda k: jax.random.permutation(k, PAGES_DEV))(jax.random.split(key_send, N_REQ))
    places = jax.vmap(lambda k: jax.random.permutation(k, PAGES_DEV))(jax.random.split(key_place, N_REQ))
    target = sends // share
    within = sends % share
    source = jnp.arange(N_REQ)[:, None]
    local_slot = places[target, source * share + within]
    return (target * PAGES_DEV + local_slot).reshape(-1).astype(jnp.int32)


def level_of(own_key, dims, cuts, low, high):
    level = 1.0
    for axis_at, parts in cuts:
        steps = jax.random.uniform(jax.random.fold_in(jax.random.fold_in(own_key, 6), axis_at), (parts,), jnp.float32, low / len(cuts), high / len(cuts))
        level = level * jnp.repeat(jnp.exp(steps), dims[axis_at] // parts).reshape((-1,) + (1,) * (len(dims) - 1 - axis_at))
    return level


def normal_values(stream_key, dims, scale, limit, cuts=(), dtype=jnp.bfloat16):
    level = level_of(stream_key, dims, cuts, -0.22, 0.18) if cuts else 1.0
    entries = jax.random.normal(stream_key, dims, jnp.float32) * scale * level
    return jnp.minimum(jnp.maximum(entries, -limit), limit).astype(dtype)


def setup_inputs(seed: int = 0) -> dict:
    streams_of = jax.random.split(jax.random.key(seed), 10)
    hidden_in = normal_values(streams_of[0], (ROWS, D), 1.0, 6.0, ((0, 128),))
    ln_gain = jnp.clip(1.0 + 0.18 * jax.random.normal(streams_of[1], (D,), jnp.float32), 0.1, 1.9)
    ln_bias = normal_values(streams_of[2], (D,), 0.5, 3.0, (), jnp.float32)
    w_query = normal_values(streams_of[3], (D, HEADS * HEAD_DIM), D ** -0.5, 0.0625, ((1, 8),))
    w_key = normal_values(streams_of[4], (D, HEADS * HEAD_DIM), D ** -0.5, 0.0625, ((1, 8),))
    w_value = normal_values(streams_of[5], (D, HEADS * HEAD_DIM), D ** -0.5, 0.0625, ((1, 8),))
    qkv_bias = draw_qkv_bias(jax.random.fold_in(streams_of[9], 71), 0)
    segment_ids = draw_segment_ids(jax.random.fold_in(streams_of[9], 71), 0)
    page_table = draw_page_table(jax.random.fold_in(streams_of[9], 71), 0)
    return {"hidden_in": hidden_in, "ln_gain": ln_gain, "ln_bias": ln_bias, "w_query": w_query, "w_key": w_key, "w_value": w_value, "qkv_bias": qkv_bias, "segment_ids": segment_ids, "page_table": page_table}


def layer_norm(rows, gain, shift):
    values = rows.astype(jnp.float32)
    center = values - lax.optimization_barrier(jnp.mean(values, axis=1, keepdims=True))
    spread = lax.optimization_barrier(jnp.mean(center * center, axis=1, keepdims=True))
    return (center * lax.rsqrt(spread + 1e-05) * gain + shift).astype(jnp.bfloat16)

def project(normed, w_query, w_key, w_value, qkv_bias, live):
    query = (jnp.dot(normed, w_query, preferred_element_type=jnp.float32) + qkv_bias[0]) * HEAD_DIM ** (-0.5)
    keys = jnp.where(live[:, None], jnp.dot(normed, w_key, preferred_element_type=jnp.float32) + qkv_bias[1], 0.0)
    values = jnp.where(live[:, None], jnp.dot(normed, w_value, preferred_element_type=jnp.float32) + qkv_bias[2], 0.0)
    return (query.astype(jnp.bfloat16), keys.astype(jnp.bfloat16), values.astype(jnp.bfloat16))

def head_rows(query_head, key_head, value_head, segments, first, last):
    count = key_head.shape[0]
    query_seg = segments[first:last]
    key_seg = segments[:count]
    query_pos = jnp.arange(first, last)
    key_pos = jnp.arange(0, count)
    visible = (query_seg[:, None] == key_seg[None, :]) & (key_seg[None, :] >= 0) & (key_pos[None, :] <= query_pos[:, None])
    scores = jnp.dot(query_head, key_head.T, preferred_element_type=jnp.float32)
    scores = jnp.where(visible, scores, -1e+30)
    top = lax.optimization_barrier(jnp.max(scores, axis=1, keepdims=True))
    weights = jnp.where(visible, jnp.exp(scores - top), 0.0)
    total = jnp.maximum(lax.optimization_barrier(jnp.sum(weights, axis=1, keepdims=True)), 1.0)
    probs = (weights / total).astype(jnp.bfloat16)
    return jnp.dot(probs, value_head, preferred_element_type=jnp.float32).astype(jnp.bfloat16)

def reference(hidden_in, ln_gain, ln_bias, w_query, w_key, w_value, qkv_bias, segment_ids, page_table):
    normed = layer_norm(hidden_in, ln_gain, ln_bias)
    query, keys, values = project(normed, w_query, w_key, w_value, qkv_bias, segment_ids >= 0)

    def split(array):
        return array.reshape(N_REQ, CAP, HEADS, HEAD_DIM).transpose(0, 2, 1, 3)

    def group(items):
        query_group, key_group, value_group, seg_group = items
        return jax.vmap(lambda a, b, c: head_rows(a, b, c, seg_group, 0, CAP))(query_group, key_group, value_group)
    attended = lax.map(group, (split(query), split(keys), split(values), segment_ids.reshape(N_REQ, CAP)))
    context = attended.transpose(0, 2, 1, 3).reshape(N_REQ * CAP, HEADS * HEAD_DIM)
    stacked = jnp.stack([keys, values]).reshape(2, SLOTS, PAGE, HEADS, HEAD_DIM)
    cache = jnp.zeros((2, SLOTS, PAGE, HEADS, HEAD_DIM), jnp.bfloat16).at[:, page_table].set(stacked)
    return (context, cache.transpose(0, 3, 1, 2, 4))
```

```python
import jax
import jax.numpy as jnp
from jax import lax
from jax.sharding import PartitionSpec as P

HEAD_DIM = 128
CHUNKS = 4


def layer_norm(rows, gain, shift):
    values = rows.astype(jnp.float32)
    center = values - jnp.mean(values, axis=1, keepdims=True)
    spread = jnp.mean(center * center, axis=1, keepdims=True)
    return (center * lax.rsqrt(spread + 1e-05) * gain + shift).astype(jnp.bfloat16)


def head_rows(query_head, key_head, value_head, segments, first, last):
    count = key_head.shape[0]
    query_pos = jnp.arange(first, last)
    key_pos = jnp.arange(0, count)
    visible = (
        (segments[:, None] == segments[None, :])
        & (segments[None, :] >= 0)
        & (key_pos[None, :] <= query_pos[:, None])
    )
    scores = jnp.dot(query_head, key_head.T, preferred_element_type=jnp.float32)
    scores = jnp.where(visible, scores, -1e30)
    top = jnp.max(scores, axis=1, keepdims=True)
    weights = jnp.where(visible, jnp.exp(scores - top), 0.0)
    total = jnp.maximum(jnp.sum(weights, axis=1, keepdims=True), 1.0)
    probs = (weights / total).astype(jnp.bfloat16)
    return jnp.dot(probs, value_head, preferred_element_type=jnp.float32).astype(jnp.bfloat16)


def attend(query, keys, values, segments):
    positions, width = query.shape
    heads = width // HEAD_DIM

    def split(array):
        return array.reshape(positions, heads, HEAD_DIM).transpose(1, 0, 2)

    query_heads, key_heads, value_heads = (split(query), split(keys), split(values))
    attended = lax.map(
        lambda items: head_rows(items[0], items[1], items[2], segments, 0, positions),
        (query_heads, key_heads, value_heads),
    )
    return attended.transpose(1, 0, 2).reshape(positions, width)


def send_pages(keys, values, page_table):
    pages = page_table.shape[0]
    positions, width = keys.shape
    page_rows = positions // pages
    heads = width // HEAD_DIM
    stacked = (
        jnp.stack([keys, values], axis=0)
        .reshape(2, pages, page_rows, heads, HEAD_DIM)
        .transpose(1, 0, 2, 3, 4)
    )
    target = page_table // pages
    local_slot = page_table % pages
    order = jnp.argsort(target, stable=True)
    moved, slots = (
        lax.all_to_all(stacked[order], "req", split_axis=0, concat_axis=0, tiled=True),
        lax.all_to_all(local_slot[order], "req", split_axis=0, concat_axis=0, tiled=True),
    )
    placed = moved[jnp.argsort(slots)]
    return placed.transpose(1, 3, 0, 2, 4)


def project_chunks(normed_local, w_query, w_key, w_value, qkv_bias, live, chunks):
    width = normed_local.shape[1] // chunks
    sums = [None, None, None]
    for c in range(chunks):
        part = lax.all_gather(
            normed_local[:, c * width : (c + 1) * width], "tp", axis=0, tiled=True
        )
        for i, w in enumerate((w_query, w_key, w_value)):
            term = jnp.dot(part, w[c * width : (c + 1) * width], preferred_element_type=jnp.float32)
            sums[i] = term if sums[i] is None else sums[i] + term
    query = (sums[0] + qkv_bias[0]) * HEAD_DIM ** (-0.5)
    keys = jnp.where(live[:, None], sums[1] + qkv_bias[1], 0.0)
    values = jnp.where(live[:, None], sums[2] + qkv_bias[2], 0.0)
    return (query.astype(jnp.bfloat16), keys.astype(jnp.bfloat16), values.astype(jnp.bfloat16))


def on_device(
    hidden_in, ln_gain, ln_bias, w_query, w_key, w_value, qkv_bias, segment_ids, page_table
):
    query, keys, values = project_chunks(
        layer_norm(hidden_in, ln_gain, ln_bias),
        w_query,
        w_key,
        w_value,
        qkv_bias,
        segment_ids >= 0,
        CHUNKS,
    )
    context = attend(query, keys, values, segment_ids)
    kv_cache = send_pages(keys, values, page_table)
    return (context, kv_cache)


def solution(mesh):
    return jax.shard_map(
        on_device,
        mesh=mesh,
        in_specs=(
            P(("req", "tp"), None),
            P(),
            P(),
            P(None, "tp"),
            P(None, "tp"),
            P(None, "tp"),
            P(None, "tp"),
            P("req"),
            P("req"),
        ),
        out_specs=(P("req", "tp"), P(None, "tp", "req", None, None)),
        check_vma=False,
    )
```

```python
import functools

import jax
import jax.numpy as jnp
from jax import lax
from jax.experimental import pallas as pl
from jax.sharding import PartitionSpec as P

HEAD_DIM = 128
CHUNKS = 2
Q_BLOCK = 256


def layer_norm(rows, gain, shift):
    values = rows.astype(jnp.float32)
    center = values - jnp.mean(values, axis=1, keepdims=True)
    spread = jnp.mean(center * center, axis=1, keepdims=True)
    return (center * lax.rsqrt(spread + 1e-05) * gain + shift).astype(jnp.bfloat16)


def attention_kernel(q_ref, k_ref, v_ref, segq_ref, segk_ref, o_ref, *, block):
    qb = pl.program_id(1)
    for b in range(k_ref.shape[0] // block):

        @pl.when(qb == b)
        def _():
            n = (b + 1) * block
            q = q_ref[...]
            k = k_ref[0:n, :]
            scores = lax.dot_general(
                q, k, (((1,), (1,)), ((), ())), preferred_element_type=jnp.float32
            )
            seg_q = segq_ref[...]
            seg_k = segk_ref[:, 0:n]
            row = b * block + lax.broadcasted_iota(jnp.int32, (block, n), 0)
            col = lax.broadcasted_iota(jnp.int32, (block, n), 1)
            visible = (seg_q == seg_k) & (seg_k >= 0) & (col <= row)
            scores = jnp.where(visible, scores, -1e30)
            top = jnp.max(scores, axis=1, keepdims=True)
            weights = jnp.where(visible, jnp.exp(scores - top), 0.0)
            total = jnp.maximum(jnp.sum(weights, axis=1, keepdims=True), 1.0)
            probs = (weights / total).astype(jnp.bfloat16)
            o_ref[...] = jnp.dot(
                probs, v_ref[0:n, :], preferred_element_type=jnp.float32
            ).astype(o_ref.dtype)


def attend(query, keys, values, segments):
    positions, width = query.shape
    heads = width // HEAD_DIM
    block = Q_BLOCK
    kernel = functools.partial(attention_kernel, block=block)
    return pl.pallas_call(
        kernel,
        grid=(heads, positions // block),
        in_specs=[
            pl.BlockSpec((block, HEAD_DIM), lambda h, i: (i, h)),
            pl.BlockSpec((positions, HEAD_DIM), lambda h, i: (0, h)),
            pl.BlockSpec((positions, HEAD_DIM), lambda h, i: (0, h)),
            pl.BlockSpec((block, 1), lambda h, i: (i, 0)),
            pl.BlockSpec((1, positions), lambda h, i: (0, 0)),
        ],
        out_specs=pl.BlockSpec((block, HEAD_DIM), lambda h, i: (i, h)),
        out_shape=jax.ShapeDtypeStruct((positions, width), query.dtype),
    )(query, keys, values, segments.reshape(positions, 1), segments.reshape(1, positions))


def send_pages(keys, values, page_table):
    pages = page_table.shape[0]
    positions, width = keys.shape
    page_rows = positions // pages
    heads = width // HEAD_DIM
    stacked = (
        jnp.stack([keys, values], axis=0)
        .reshape(2, pages, page_rows, heads, HEAD_DIM)
        .transpose(1, 0, 2, 3, 4)
    )
    target = page_table // pages
    local_slot = page_table % pages
    order = jnp.argsort(target, stable=True)
    moved, slots = (
        lax.all_to_all(stacked[order], "req", split_axis=0, concat_axis=0, tiled=True),
        lax.all_to_all(local_slot[order], "req", split_axis=0, concat_axis=0, tiled=True),
    )
    placed = moved[jnp.argsort(slots)]
    return placed.transpose(1, 3, 0, 2, 4)


def project_chunks(normed_local, w_query, w_key, w_value, qkv_bias, live, chunks):
    width = normed_local.shape[1] // chunks
    sums = [None, None, None]
    for c in range(chunks):
        part = lax.all_gather(
            normed_local[:, c * width : (c + 1) * width], "tp", axis=0, tiled=True
        )
        for i, w in enumerate((w_query, w_key, w_value)):
            term = jnp.dot(part, w[c * width : (c + 1) * width], preferred_element_type=jnp.float32)
            sums[i] = term if sums[i] is None else sums[i] + term
    query = (sums[0] + qkv_bias[0]) * HEAD_DIM ** (-0.5)
    keys = jnp.where(live[:, None], sums[1] + qkv_bias[1], 0.0)
    values = jnp.where(live[:, None], sums[2] + qkv_bias[2], 0.0)
    return (query.astype(jnp.bfloat16), keys.astype(jnp.bfloat16), values.astype(jnp.bfloat16))


def on_device(
    hidden_in, ln_gain, ln_bias, w_query, w_key, w_value, qkv_bias, segment_ids, page_table
):
    query, keys, values = project_chunks(
        layer_norm(hidden_in, ln_gain, ln_bias),
        w_query,
        w_key,
        w_value,
        qkv_bias,
        segment_ids >= 0,
        CHUNKS,
    )
    context = attend(query, keys, values, segment_ids)
    kv_cache = send_pages(keys, values, page_table)
    return (context, kv_cache)


def solution(mesh):
    return jax.shard_map(
        on_device,
        mesh=mesh,
        in_specs=(
            P(("req", "tp"), None),
            P(),
            P(),
            P(None, "tp"),
            P(None, "tp"),
            P(None, "tp"),
            P(None, "tp"),
            P("req"),
            P("req"),
        ),
        out_specs=(P("req", "tp"), P(None, "tp", "req", None, None)),
        check_vma=False,
    )
```

```python
import functools

import jax
import jax.numpy as jnp
from jax import lax
from jax.experimental import pallas as pl
from jax.sharding import PartitionSpec as P

HEAD_DIM = 128
SPLIT = 6144
Q_BLOCK = 256


def layer_norm(rows, gain, shift):
    values = rows.astype(jnp.float32)
    center = values - jnp.mean(values, axis=1, keepdims=True)
    spread = jnp.mean(center * center, axis=1, keepdims=True)
    return (center * lax.rsqrt(spread + 1e-05) * gain + shift).astype(jnp.bfloat16)


def attention_kernel(q_ref, k_ref, v_ref, segq_ref, segk_ref, o_ref, *, block):
    qb = pl.program_id(1)
    for b in range(k_ref.shape[0] // block):

        @pl.when(qb == b)
        def _():
            n = (b + 1) * block
            q = q_ref[...]
            k = k_ref[0:n, :]
            scores = lax.dot_general(
                q, k, (((1,), (1,)), ((), ())), preferred_element_type=jnp.float32
            )
            seg_q = segq_ref[...]
            seg_k = segk_ref[:, 0:n]
            row = b * block + lax.broadcasted_iota(jnp.int32, (block, n), 0)
            col = lax.broadcasted_iota(jnp.int32, (block, n), 1)
            visible = (seg_q == seg_k) & (seg_k >= 0) & (col <= row)
            scores = jnp.where(visible, scores, -1e30)
            top = jnp.max(scores, axis=1, keepdims=True)
            weights = jnp.where(visible, jnp.exp(scores - top), 0.0)
            total = jnp.maximum(jnp.sum(weights, axis=1, keepdims=True), 1.0)
            probs = (weights * (1.0 / total)).astype(jnp.bfloat16)
            o_ref[...] = jnp.dot(
                probs, v_ref[0:n, :], preferred_element_type=jnp.float32
            ).astype(o_ref.dtype)


def attend(query, keys, values, segments):
    positions, width = query.shape
    heads = width // HEAD_DIM
    block = Q_BLOCK
    kernel = functools.partial(attention_kernel, block=block)
    return pl.pallas_call(
        kernel,
        grid=(heads, positions // block),
        in_specs=[
            pl.BlockSpec((block, HEAD_DIM), lambda h, i: (i, h)),
            pl.BlockSpec((positions, HEAD_DIM), lambda h, i: (0, h)),
            pl.BlockSpec((positions, HEAD_DIM), lambda h, i: (0, h)),
            pl.BlockSpec((block, 1), lambda h, i: (i, 0)),
            pl.BlockSpec((1, positions), lambda h, i: (0, 0)),
        ],
        out_specs=pl.BlockSpec((block, HEAD_DIM), lambda h, i: (i, h)),
        out_shape=jax.ShapeDtypeStruct((positions, width), query.dtype),
    )(query, keys, values, segments.reshape(positions, 1), segments.reshape(1, positions))


def send_pages(keys, values, page_table):
    pages = page_table.shape[0]
    positions, width = keys.shape
    page_rows = positions // pages
    heads = width // HEAD_DIM
    stacked = (
        jnp.stack([keys, values], axis=0)
        .reshape(2, pages, page_rows, heads, HEAD_DIM)
        .transpose(1, 0, 2, 3, 4)
    )
    target = page_table // pages
    local_slot = page_table % pages
    order = jnp.argsort(target, stable=True)
    moved, slots = (
        lax.all_to_all(stacked[order], "req", split_axis=0, concat_axis=0, tiled=True),
        lax.all_to_all(local_slot[order], "req", split_axis=0, concat_axis=0, tiled=True),
    )
    placed = moved[jnp.argsort(slots)]
    return placed.transpose(1, 3, 0, 2, 4)


def project_chunks(normed_local, w_query, w_key, w_value, qkv_bias, live, bounds):
    sums = [None, None, None]
    for lo, hi in zip(bounds[:-1], bounds[1:]):
        part = lax.all_gather(normed_local[:, lo:hi], "tp", axis=0, tiled=True)
        for i, w in enumerate((w_query, w_key, w_value)):
            term = jnp.dot(part, w[lo:hi], preferred_element_type=jnp.float32)
            sums[i] = term if sums[i] is None else sums[i] + term
        if hi < bounds[-1]:
            sums = list(lax.optimization_barrier(tuple(sums)))
    query = (sums[0] + qkv_bias[0]) * HEAD_DIM ** (-0.5)
    keys = jnp.where(live[:, None], sums[1] + qkv_bias[1], 0.0)
    values = jnp.where(live[:, None], sums[2] + qkv_bias[2], 0.0)
    return (query.astype(jnp.bfloat16), keys.astype(jnp.bfloat16), values.astype(jnp.bfloat16))


def on_device(
    hidden_in, ln_gain, ln_bias, w_query, w_key, w_value, qkv_bias, segment_ids, page_table
):
    query, keys, values = project_chunks(
        layer_norm(hidden_in, ln_gain, ln_bias),
        w_query,
        w_key,
        w_value,
        qkv_bias,
        segment_ids >= 0,
        (0, SPLIT, hidden_in.shape[1]),
    )
    context = attend(query, keys, values, segment_ids)
    kv_cache = send_pages(keys, values, page_table)
    return (context, kv_cache)


def solution(mesh):
    return jax.shard_map(
        on_device,
        mesh=mesh,
        in_specs=(
            P(("req", "tp"), None),
            P(),
            P(),
            P(None, "tp"),
            P(None, "tp"),
            P(None, "tp"),
            P(None, "tp"),
            P("req"),
            P("req"),
        ),
        out_specs=(P("req", "tp"), P(None, "tp", "req", None, None)),
        check_vma=False,
    )
```

```python
import functools

import jax
import jax.numpy as jnp
from jax import lax
from jax.experimental import pallas as pl
from jax.sharding import PartitionSpec as P

HEAD_DIM = 128
SPLIT = 6656
Q_BLOCK = 256


def layer_norm(rows, gain, shift):
    values = rows.astype(jnp.float32)
    center = values - jnp.mean(values, axis=1, keepdims=True)
    spread = jnp.mean(center * center, axis=1, keepdims=True)
    return (center * lax.rsqrt(spread + 1e-05) * gain + shift).astype(jnp.bfloat16)


def attention_kernel(q_ref, k_ref, v_ref, lo_ref, hi_ref, o_ref, *, block):
    qb = pl.program_id(0)
    for b in range(k_ref.shape[0] // block):

        @pl.when(qb == b)
        def _():
            n = (b + 1) * block
            col = lax.broadcasted_iota(jnp.int32, (block, n), 1)
            lo = lo_ref[...]
            hi = hi_ref[...]
            visible = (col >= lo) & (col <= hi)
            live = hi >= 0
            for h in range(q_ref.shape[1] // HEAD_DIM):
                cols = slice(h * HEAD_DIM, (h + 1) * HEAD_DIM)
                scores = lax.dot_general(
                    q_ref[:, cols],
                    k_ref[0:n, cols],
                    (((1,), (1,)), ((), ())),
                    preferred_element_type=jnp.float32,
                )
                scores = jnp.where(visible, scores, -1e30)
                top = jnp.max(scores, axis=1, keepdims=True)
                weights = jnp.exp(scores - top)
                total = jnp.maximum(jnp.sum(weights, axis=1, keepdims=True), 1.0)
                scale = jnp.where(live, 1.0 / total, 0.0)
                probs = (weights * scale).astype(jnp.bfloat16)
                o_ref[:, cols] = jnp.dot(
                    probs, v_ref[0:n, cols], preferred_element_type=jnp.float32
                ).astype(o_ref.dtype)


def attend(query, keys, values, segments):
    positions, width = query.shape
    block = Q_BLOCK
    position = jnp.arange(positions, dtype=jnp.int32)
    first = jnp.concatenate([jnp.ones((1,), bool), segments[1:] != segments[:-1]])
    lo = lax.cummax(jnp.where(first, position, 0), axis=0)
    hi = jnp.where(segments >= 0, position, -1)
    kernel = functools.partial(attention_kernel, block=block)
    return pl.pallas_call(
        kernel,
        grid=(positions // block,),
        in_specs=[
            pl.BlockSpec((block, width), lambda i: (i, 0)),
            pl.BlockSpec((positions, width), lambda i: (0, 0)),
            pl.BlockSpec((positions, width), lambda i: (0, 0)),
            pl.BlockSpec((block, 1), lambda i: (i, 0)),
            pl.BlockSpec((block, 1), lambda i: (i, 0)),
        ],
        out_specs=pl.BlockSpec((block, width), lambda i: (i, 0)),
        out_shape=jax.ShapeDtypeStruct((positions, width), query.dtype),
    )(query, keys, values, lo.reshape(positions, 1), hi.reshape(positions, 1))


def send_pages(keys, values, page_table):
    pages = page_table.shape[0]
    positions, width = keys.shape
    page_rows = positions // pages
    heads = width // HEAD_DIM
    stacked = (
        jnp.stack([keys, values], axis=0)
        .reshape(2, pages, page_rows, heads, HEAD_DIM)
        .transpose(1, 0, 2, 3, 4)
    )
    target = page_table // pages
    local_slot = page_table % pages
    order = jnp.argsort(target, stable=True)
    slots = lax.all_to_all(local_slot[order], "req", split_axis=0, concat_axis=0, tiled=True)
    inverse = jnp.argsort(slots)
    moved = lax.all_to_all(stacked[order], "req", split_axis=0, concat_axis=0, tiled=True)
    return moved[inverse].transpose(1, 3, 0, 2, 4)


def project_chunks(normed_local, w_query, w_key, w_value, qkv_bias, live, bounds):
    sums = [None, None, None]
    for lo, hi in zip(bounds[:-1], bounds[1:]):
        part = lax.all_gather(normed_local[:, lo:hi], "tp", axis=0, tiled=True)
        for i, w in enumerate((w_value, w_key, w_query)):
            term = jnp.dot(part, w[lo:hi], preferred_element_type=jnp.float32)
            sums[2 - i] = term if sums[2 - i] is None else sums[2 - i] + term
        if hi < bounds[-1]:
            sums = list(lax.optimization_barrier(tuple(sums)))
    query = (sums[0] + qkv_bias[0]) * HEAD_DIM ** (-0.5)
    keys = jnp.where(live[:, None], sums[1] + qkv_bias[1], 0.0)
    values = jnp.where(live[:, None], sums[2] + qkv_bias[2], 0.0)
    return (query.astype(jnp.bfloat16), keys.astype(jnp.bfloat16), values.astype(jnp.bfloat16))


def on_device(
    hidden_in, ln_gain, ln_bias, w_query, w_key, w_value, qkv_bias, segment_ids, page_table
):
    bounds = (0, SPLIT, hidden_in.shape[1])
    query, keys, values = project_chunks(
        layer_norm(hidden_in, ln_gain, ln_bias),
        w_query,
        w_key,
        w_value,
        qkv_bias,
        segment_ids >= 0,
        bounds,
    )
    context = attend(query, keys, values, segment_ids)
    kv_cache = send_pages(keys, values, page_table)
    return (context, kv_cache)


def solution(mesh):
    return jax.shard_map(
        on_device,
        mesh=mesh,
        in_specs=(
            P(("req", "tp"), None),
            P(),
            P(),
            P(None, "tp"),
            P(None, "tp"),
            P(None, "tp"),
            P(None, "tp"),
            P("req"),
            P("req"),
        ),
        out_specs=(P("req", "tp"), P(None, "tp", "req", None, None)),
        check_vma=False,
    )
```

```python
import functools

import jax
import jax.numpy as jnp
from jax import lax
from jax.experimental import pallas as pl
from jax.sharding import PartitionSpec as P

HEAD_DIM = 128
Q_BLOCK = 256


def layer_norm(rows, gain, shift):
    values = rows.astype(jnp.float32)
    center = values - jnp.mean(values, axis=1, keepdims=True)
    spread = jnp.mean(center * center, axis=1, keepdims=True)
    return (center * lax.rsqrt(spread + 1e-05) * gain + shift).astype(jnp.bfloat16)


def attention_kernel(q_ref, k_ref, v_ref, lo_ref, hi_ref, o_ref, *, block):
    qb = pl.program_id(0)
    for b in range(k_ref.shape[0] // block):

        @pl.when(qb == b)
        def _():
            n = (b + 1) * block
            col = lax.broadcasted_iota(jnp.int32, (block, n), 1)
            lo = lo_ref[...]
            hi = hi_ref[...]
            visible = (col >= lo) & (col <= hi)
            live = hi >= 0
            for h in range(q_ref.shape[1] // HEAD_DIM):
                cols = slice(h * HEAD_DIM, (h + 1) * HEAD_DIM)
                scores = lax.dot_general(
                    q_ref[:, cols],
                    k_ref[0:n, cols],
                    (((1,), (1,)), ((), ())),
                    preferred_element_type=jnp.float32,
                )
                scores = jnp.where(visible, scores, -1e30)
                top = jnp.max(scores, axis=1, keepdims=True)
                weights = jnp.exp(scores - top)
                total = jnp.maximum(jnp.sum(weights, axis=1, keepdims=True), 1.0)
                scale = jnp.where(live, 1.0 / total, 0.0)
                probs = (weights * scale).astype(jnp.bfloat16)
                o_ref[:, cols] = jnp.dot(
                    probs, v_ref[0:n, cols], preferred_element_type=jnp.float32
                ).astype(o_ref.dtype)


def attend(query, keys, values, segments):
    positions, width = query.shape
    block = Q_BLOCK
    position = jnp.arange(positions, dtype=jnp.int32)
    first = jnp.concatenate([jnp.ones((1,), bool), segments[1:] != segments[:-1]])
    lo = lax.cummax(jnp.where(first, position, 0), axis=0)
    hi = jnp.where(segments >= 0, position, -1)
    kernel = functools.partial(attention_kernel, block=block)
    return pl.pallas_call(
        kernel,
        grid=(positions // block,),
        in_specs=[
            pl.BlockSpec((block, width), lambda i: (i, 0)),
            pl.BlockSpec((positions, width), lambda i: (0, 0)),
            pl.BlockSpec((positions, width), lambda i: (0, 0)),
            pl.BlockSpec((block, 1), lambda i: (i, 0)),
            pl.BlockSpec((block, 1), lambda i: (i, 0)),
        ],
        out_specs=pl.BlockSpec((block, width), lambda i: (i, 0)),
        out_shape=jax.ShapeDtypeStruct((positions, width), query.dtype),
    )(query, keys, values, lo.reshape(positions, 1), hi.reshape(positions, 1))


def send_pages(keys, values, page_table):
    pages = page_table.shape[0]
    positions, width = keys.shape
    page_rows = positions // pages
    heads = width // HEAD_DIM
    stacked = (
        jnp.stack([keys, values], axis=0)
        .reshape(2, pages, page_rows, heads, HEAD_DIM)
        .transpose(1, 0, 2, 3, 4)
    )
    target = page_table // pages
    local_slot = page_table % pages
    order = jnp.argsort(target, stable=True)
    slots = lax.all_to_all(local_slot[order], "req", split_axis=0, concat_axis=0, tiled=True)
    inverse = jnp.argsort(slots)
    moved = lax.all_to_all(stacked[order], "req", split_axis=0, concat_axis=0, tiled=True)
    return moved[inverse].transpose(1, 3, 0, 2, 4)


def project_chunks(normed_local, w_query, w_key, w_value, qkv_bias, live, bounds):
    sums = [None, None, None]
    for lo, hi in zip(bounds[:-1], bounds[1:]):
        part = lax.all_gather(normed_local[:, lo:hi], "tp", axis=0, tiled=True)
        for i, w in enumerate((w_query, w_key, w_value)):
            term = jnp.dot(part, w[lo:hi], preferred_element_type=jnp.float32)
            sums[i] = term if sums[i] is None else sums[i] + term
        if hi < bounds[-1]:
            sums = list(lax.optimization_barrier(tuple(sums)))
    query = (sums[0] + qkv_bias[0]) * HEAD_DIM ** (-0.5)
    keys = jnp.where(live[:, None], sums[1] + qkv_bias[1], 0.0)
    values = jnp.where(live[:, None], sums[2] + qkv_bias[2], 0.0)
    return (query.astype(jnp.bfloat16), keys.astype(jnp.bfloat16), values.astype(jnp.bfloat16))


def on_device(
    hidden_in, ln_gain, ln_bias, w_query, w_key, w_value, qkv_bias, segment_ids, page_table
):
    query, keys, values = project_chunks(
        layer_norm(hidden_in, ln_gain, ln_bias),
        w_query,
        w_key,
        w_value,
        qkv_bias,
        segment_ids >= 0,
        (0, hidden_in.shape[1]),
    )
    context = attend(query, keys, values, segment_ids)
    kv_cache = send_pages(keys, values, page_table)
    return (context, kv_cache)


def solution(mesh):
    return jax.shard_map(
        on_device,
        mesh=mesh,
        in_specs=(
            P(("req", "tp"), None),
            P(),
            P(),
            P(None, "tp"),
            P(None, "tp"),
            P(None, "tp"),
            P(None, "tp"),
            P("req"),
            P("req"),
        ),
        out_specs=(P("req", "tp"), P(None, "tp", "req", None, None)),
        check_vma=False,
    )
```

```python
import functools

import jax
import jax.numpy as jnp
from jax import lax
from jax.experimental import pallas as pl
from jax.sharding import PartitionSpec as P

HEAD_DIM = 128
LATE_ROWS = 16
Q_BLOCK = 256


def layer_norm(rows, gain, shift):
    values = rows.astype(jnp.float32)
    center = values - jnp.mean(values, axis=1, keepdims=True)
    spread = jnp.mean(center * center, axis=1, keepdims=True)
    return (center * lax.rsqrt(spread + 1e-05) * gain + shift).astype(jnp.bfloat16)


def attention_kernel(q_ref, k_ref, v_ref, lo_ref, hi_ref, o_ref, *, block):
    qb = pl.program_id(0)
    for b in range(k_ref.shape[0] // block):

        @pl.when(qb == b)
        def _():
            n = (b + 1) * block
            col = lax.broadcasted_iota(jnp.int32, (block, n), 1)
            lo = lo_ref[...]
            hi = hi_ref[...]
            visible = (col >= lo) & (col <= hi)
            live = hi >= 0
            for h in range(q_ref.shape[1] // HEAD_DIM):
                cols = slice(h * HEAD_DIM, (h + 1) * HEAD_DIM)
                scores = lax.dot_general(
                    q_ref[:, cols],
                    k_ref[0:n, cols],
                    (((1,), (1,)), ((), ())),
                    preferred_element_type=jnp.float32,
                )
                scores = jnp.where(visible, scores, -1e30)
                top = jnp.max(scores, axis=1, keepdims=True)
                weights = jnp.exp(scores - top)
                total = jnp.maximum(jnp.sum(weights, axis=1, keepdims=True), 1.0)
                scale = jnp.where(live, 1.0 / total, 0.0)
                probs = (weights * scale).astype(jnp.bfloat16)
                o_ref[:, cols] = jnp.dot(
                    probs, v_ref[0:n, cols], preferred_element_type=jnp.float32
                ).astype(o_ref.dtype)


def attend(query, keys, values, segments):
    positions, width = query.shape
    block = Q_BLOCK
    position = jnp.arange(positions, dtype=jnp.int32)
    first = jnp.concatenate([jnp.ones((1,), bool), segments[1:] != segments[:-1]])
    lo = lax.cummax(jnp.where(first, position, 0), axis=0)
    hi = jnp.where(segments >= 0, position, -1)
    kernel = functools.partial(attention_kernel, block=block)
    return pl.pallas_call(
        kernel,
        grid=(positions // block,),
        in_specs=[
            pl.BlockSpec((block, width), lambda i: (i, 0)),
            pl.BlockSpec((positions, width), lambda i: (0, 0)),
            pl.BlockSpec((positions, width), lambda i: (0, 0)),
            pl.BlockSpec((block, 1), lambda i: (i, 0)),
            pl.BlockSpec((block, 1), lambda i: (i, 0)),
        ],
        out_specs=pl.BlockSpec((block, width), lambda i: (i, 0)),
        out_shape=jax.ShapeDtypeStruct((positions, width), query.dtype),
    )(query, keys, values, lo.reshape(positions, 1), hi.reshape(positions, 1))


def send_pages(keys, values, page_table):
    pages = page_table.shape[0]
    positions, width = keys.shape
    page_rows = positions // pages
    heads = width // HEAD_DIM
    stacked = (
        jnp.stack([keys, values], axis=0)
        .reshape(2, pages, page_rows, heads, HEAD_DIM)
        .transpose(1, 0, 2, 3, 4)
    )
    target = page_table // pages
    local_slot = page_table % pages
    order = jnp.argsort(target, stable=True)
    slots = lax.all_to_all(local_slot[order], "req", split_axis=0, concat_axis=0, tiled=True)
    inverse = jnp.argsort(slots)
    moved = lax.all_to_all(stacked[order], "req", split_axis=0, concat_axis=0, tiled=True)
    return moved[inverse].transpose(1, 3, 0, 2, 4)


def project_rows(normed, w_query, w_key, w_value, qkv_bias, live):
    keys = jnp.where(
        live[:, None],
        jnp.dot(normed, w_key, preferred_element_type=jnp.float32) + qkv_bias[1],
        0.0,
    ).astype(jnp.bfloat16)
    values = jnp.where(
        live[:, None],
        jnp.dot(normed, w_value, preferred_element_type=jnp.float32) + qkv_bias[2],
        0.0,
    ).astype(jnp.bfloat16)
    query = (
        (jnp.dot(normed, w_query, preferred_element_type=jnp.float32) + qkv_bias[0])
        * HEAD_DIM ** (-0.5)
    ).astype(jnp.bfloat16)
    return [query, keys, values]


def project_split(normed_local, w_query, w_key, w_value, qkv_bias, live):
    rows = normed_local.shape[0]
    early = rows - LATE_ROWS
    parts = lax.axis_size("tp")
    me = lax.axis_index("tp")
    first = lax.all_gather(normed_local[:early], "tp", axis=0, tiled=True)
    received = [normed_local[early:]] + [
        lax.ppermute(
            normed_local[early:], "tp", [(i, (i + s) % parts) for i in range(parts)]
        )
        for s in range(1, parts)
    ]
    late = jnp.take(jnp.stack(received), (me - jnp.arange(parts)) % parts, axis=0)
    late = late.reshape(parts * LATE_ROWS, -1)
    live_blocks = live.reshape(parts, rows)
    early_out = project_rows(
        first, w_query, w_key, w_value, qkv_bias, live_blocks[:, :early].reshape(-1)
    )
    late_out = project_rows(
        late, w_query, w_key, w_value, qkv_bias, live_blocks[:, early:].reshape(-1)
    )
    return [
        jnp.concatenate(
            [a.reshape(parts, early, -1), b.reshape(parts, LATE_ROWS, -1)], axis=1
        ).reshape(parts * rows, -1)
        for a, b in zip(early_out, late_out)
    ]


def on_device(
    hidden_in, ln_gain, ln_bias, w_query, w_key, w_value, qkv_bias, segment_ids, page_table
):
    query, keys, values = project_split(
        layer_norm(hidden_in, ln_gain, ln_bias),
        w_query,
        w_key,
        w_value,
        qkv_bias,
        segment_ids >= 0,
    )
    context = attend(query, keys, values, segment_ids)
    kv_cache = send_pages(keys, values, page_table)
    return (context, kv_cache)


def solution(mesh):
    return jax.shard_map(
        on_device,
        mesh=mesh,
        in_specs=(
            P(("req", "tp"), None),
            P(),
            P(),
            P(None, "tp"),
            P(None, "tp"),
            P(None, "tp"),
            P(None, "tp"),
            P("req"),
            P("req"),
        ),
        out_specs=(P("req", "tp"), P(None, "tp", "req", None, None)),
        check_vma=False,
    )
```

```python
import functools

import jax
import jax.numpy as jnp
from jax import lax
from jax.experimental import pallas as pl
from jax.sharding import PartitionSpec as P

HEAD_DIM = 128
Q_BLOCK = 256


def layer_norm(rows, gain, shift):
    values = rows.astype(jnp.float32)
    center = values - jnp.mean(values, axis=1, keepdims=True)
    spread = jnp.mean(center * center, axis=1, keepdims=True)
    return (center * lax.rsqrt(spread + 1e-05) * gain + shift).astype(jnp.bfloat16)


def attention_kernel(q_ref, k_ref, v_ref, lo_ref, hi_ref, o_ref, *, block):
    qb = pl.program_id(0)
    for b in range(k_ref.shape[0] // block):

        @pl.when(qb == b)
        def _():
            n = (b + 1) * block
            col = lax.broadcasted_iota(jnp.int32, (block, n), 1)
            lo = lo_ref[...]
            hi = hi_ref[...]
            visible = (col >= lo) & (col <= hi)
            live = hi >= 0
            for h in range(q_ref.shape[1] // HEAD_DIM):
                cols = slice(h * HEAD_DIM, (h + 1) * HEAD_DIM)
                scores = lax.dot_general(
                    q_ref[:, cols],
                    k_ref[0:n, cols],
                    (((1,), (1,)), ((), ())),
                    preferred_element_type=jnp.float32,
                )
                scores = jnp.where(visible, scores, -1e30)
                top = jnp.max(scores, axis=1, keepdims=True)
                weights = jnp.exp(scores - top)
                total = jnp.maximum(jnp.sum(weights, axis=1, keepdims=True), 1.0)
                scale = jnp.where(live, 1.0 / total, 0.0)
                probs = (weights * scale).astype(jnp.bfloat16)
                o_ref[:, cols] = jnp.dot(
                    probs, v_ref[0:n, cols], preferred_element_type=jnp.float32
                ).astype(o_ref.dtype)


def attend(query, kv, segments):
    positions, width = query.shape
    block = Q_BLOCK
    position = jnp.arange(positions, dtype=jnp.int32)
    first = jnp.concatenate([jnp.ones((1,), bool), segments[1:] != segments[:-1]])
    lo = lax.cummax(jnp.where(first, position, 0), axis=0)
    hi = jnp.where(segments >= 0, position, -1)
    kernel = functools.partial(attention_kernel, block=block)
    return pl.pallas_call(
        kernel,
        grid=(positions // block,),
        in_specs=[
            pl.BlockSpec((block, width), lambda i: (i, 0)),
            pl.BlockSpec((positions, width), lambda i: (0, 0)),
            pl.BlockSpec((positions, width), lambda i: (0, 1)),
            pl.BlockSpec((block, 1), lambda i: (i, 0)),
            pl.BlockSpec((block, 1), lambda i: (i, 0)),
        ],
        out_specs=pl.BlockSpec((block, width), lambda i: (i, 0)),
        out_shape=jax.ShapeDtypeStruct((positions, width), query.dtype),
    )(query, kv, kv, lo.reshape(positions, 1), hi.reshape(positions, 1))


def send_pages(kv, page_table):
    pages = page_table.shape[0]
    positions, width = kv.shape
    page_rows = positions // pages
    heads = width // (2 * HEAD_DIM)
    stacked = kv.reshape(pages, page_rows, 2, heads, HEAD_DIM).transpose(0, 2, 1, 3, 4)
    target = page_table // pages
    local_slot = page_table % pages
    order = jnp.argsort(target, stable=True)
    slots = lax.all_to_all(local_slot[order], "req", split_axis=0, concat_axis=0, tiled=True)
    inverse = jnp.argsort(slots)
    moved = lax.all_to_all(stacked[order], "req", split_axis=0, concat_axis=0, tiled=True)
    return moved[inverse].transpose(1, 3, 0, 2, 4)


def project_all(normed_local, w_query, w_key, w_value, qkv_bias, live):
    w_kv = jnp.concatenate([w_key, w_value], axis=1)
    normed = lax.all_gather(normed_local, "tp", axis=0, tiled=True)
    bias_kv = jnp.concatenate([qkv_bias[1], qkv_bias[2]])
    kv = jnp.where(
        live[:, None], jnp.dot(normed, w_kv, preferred_element_type=jnp.float32) + bias_kv, 0.0
    ).astype(jnp.bfloat16)
    query = (
        (jnp.dot(normed, w_query, preferred_element_type=jnp.float32) + qkv_bias[0])
        * HEAD_DIM ** (-0.5)
    ).astype(jnp.bfloat16)
    return (query, kv)


def on_device(
    hidden_in, ln_gain, ln_bias, w_query, w_key, w_value, qkv_bias, segment_ids, page_table
):
    query, kv = project_all(
        layer_norm(hidden_in, ln_gain, ln_bias),
        w_query,
        w_key,
        w_value,
        qkv_bias,
        segment_ids >= 0,
    )
    context = attend(query, kv, segment_ids)
    kv_cache = send_pages(kv, page_table)
    return (context, kv_cache)


def solution(mesh):
    return jax.shard_map(
        on_device,
        mesh=mesh,
        in_specs=(
            P(("req", "tp"), None),
            P(),
            P(),
            P(None, "tp"),
            P(None, "tp"),
            P(None, "tp"),
            P(None, "tp"),
            P("req"),
            P("req"),
        ),
        out_specs=(P("req", "tp"), P(None, "tp", "req", None, None)),
        check_vma=False,
    )
```

```python
import functools

import jax
import jax.numpy as jnp
from jax import lax
from jax.experimental import pallas as pl
from jax.sharding import PartitionSpec as P

HEAD_DIM = 128
Q_BLOCK = 256


def layer_norm(rows, gain, shift):
    values = rows.astype(jnp.float32)
    center = values - jnp.mean(values, axis=1, keepdims=True)
    spread = jnp.mean(center * center, axis=1, keepdims=True)
    return (center * lax.rsqrt(spread + 1e-05) * gain + shift).astype(jnp.bfloat16)


def attention_kernel(q_ref, k_ref, v_ref, lo_ref, hi_ref, o_ref, *, block):
    qb = pl.program_id(0)
    for b in range(k_ref.shape[0] // block):

        @pl.when(qb == b)
        def _():
            n = (b + 1) * block
            col = lax.broadcasted_iota(jnp.int32, (block, n), 1)
            lo = lo_ref[...]
            hi = hi_ref[...]
            visible = (col >= lo) & (col <= hi)
            live = hi >= 0
            for h in range(q_ref.shape[1] // HEAD_DIM):
                cols = slice(h * HEAD_DIM, (h + 1) * HEAD_DIM)
                scores = lax.dot_general(
                    q_ref[:, cols],
                    k_ref[0:n, cols],
                    (((1,), (1,)), ((), ())),
                    preferred_element_type=jnp.float32,
                )
                scores = jnp.where(visible, scores, -1e30)
                top = jnp.max(scores, axis=1, keepdims=True)
                weights = jnp.exp(scores - top)
                total = jnp.maximum(jnp.sum(weights, axis=1, keepdims=True), 1.0)
                scale = jnp.where(live, 1.0 / total, 0.0)
                probs = (weights * scale).astype(jnp.bfloat16)
                o_ref[:, cols] = jnp.dot(
                    probs, v_ref[0:n, cols], preferred_element_type=jnp.float32
                ).astype(o_ref.dtype)


def attend(query, kv, segments):
    positions, width = query.shape
    block = Q_BLOCK
    position = jnp.arange(positions, dtype=jnp.int32)
    first = jnp.concatenate([jnp.ones((1,), bool), segments[1:] != segments[:-1]])
    lo = lax.cummax(jnp.where(first, position, 0), axis=0)
    hi = jnp.where(segments >= 0, position, -1)
    kernel = functools.partial(attention_kernel, block=block)
    return pl.pallas_call(
        kernel,
        grid=(positions // block,),
        in_specs=[
            pl.BlockSpec((block, width), lambda i: (i, 0)),
            pl.BlockSpec((positions, width), lambda i: (0, 0)),
            pl.BlockSpec((positions, width), lambda i: (0, 1)),
            pl.BlockSpec((block, 1), lambda i: (i, 0)),
            pl.BlockSpec((block, 1), lambda i: (i, 0)),
        ],
        out_specs=pl.BlockSpec((block, width), lambda i: (i, 0)),
        out_shape=jax.ShapeDtypeStruct((positions, width), query.dtype),
    )(query, kv, kv, lo.reshape(positions, 1), hi.reshape(positions, 1))


def send_pages(kv, page_table):
    pages = page_table.shape[0]
    positions, width = kv.shape
    page_rows = positions // pages
    heads = width // (2 * HEAD_DIM)
    paged = kv.reshape(pages, page_rows, width)
    target = page_table // pages
    local_slot = page_table % pages
    order = jnp.argsort(target, stable=True)
    slots = lax.all_to_all(local_slot[order], "req", split_axis=0, concat_axis=0, tiled=True)
    inverse = jnp.argsort(slots)
    moved = lax.all_to_all(paged[order], "req", split_axis=0, concat_axis=0, tiled=True)
    placed = moved[inverse].reshape(pages, page_rows, 2, heads, HEAD_DIM)
    return placed.transpose(2, 3, 0, 1, 4)


def project_all(normed_local, w_query, w_key, w_value, qkv_bias, live):
    w_kv = jnp.concatenate([w_key, w_value], axis=1)
    normed = lax.all_gather(normed_local, "tp", axis=0, tiled=True)
    bias_kv = jnp.concatenate([qkv_bias[1], qkv_bias[2]])
    kv = jnp.where(
        live[:, None], jnp.dot(normed, w_kv, preferred_element_type=jnp.float32) + bias_kv, 0.0
    ).astype(jnp.bfloat16)
    query = (
        (jnp.dot(normed, w_query, preferred_element_type=jnp.float32) + qkv_bias[0])
        * HEAD_DIM ** (-0.5)
    ).astype(jnp.bfloat16)
    return (query, kv)


def on_device(
    hidden_in, ln_gain, ln_bias, w_query, w_key, w_value, qkv_bias, segment_ids, page_table
):
    query, kv = project_all(
        layer_norm(hidden_in, ln_gain, ln_bias),
        w_query,
        w_key,
        w_value,
        qkv_bias,
        segment_ids >= 0,
    )
    context = attend(query, kv, segment_ids)
    kv_cache = send_pages(kv, page_table)
    return (context, kv_cache)


def solution(mesh):
    return jax.shard_map(
        on_device,
        mesh=mesh,
        in_specs=(
            P(("req", "tp"), None),
            P(),
            P(),
            P(None, "tp"),
            P(None, "tp"),
            P(None, "tp"),
            P(None, "tp"),
            P("req"),
            P("req"),
        ),
        out_specs=(P("req", "tp"), P(None, "tp", "req", None, None)),
        check_vma=False,
    )
```

```python
import functools

import jax
import jax.numpy as jnp
from jax import lax
from jax.experimental import pallas as pl
from jax.experimental.pallas import tpu as pltpu
from jax.sharding import PartitionSpec as P

HEAD_DIM = 128
Q_BLOCK = 256


def layer_norm(rows, gain, shift):
    values = rows.astype(jnp.float32)
    center = values - jnp.mean(values, axis=1, keepdims=True)
    spread = jnp.mean(center * center, axis=1, keepdims=True)
    return (center * lax.rsqrt(spread + 1e-05) * gain + shift).astype(jnp.bfloat16)


def attention_kernel(q_ref, k_ref, v_ref, lo_ref, hi_ref, o_ref, *, block):
    qb = pl.program_id(0)
    for b in range(k_ref.shape[0] // block):

        @pl.when(qb == b)
        def _():
            n = (b + 1) * block
            col = lax.broadcasted_iota(jnp.int32, (block, n), 1)
            lo = lo_ref[...]
            hi = hi_ref[...]
            visible = (col >= lo) & (col <= hi)
            live = hi >= 0
            for h in range(q_ref.shape[1] // HEAD_DIM):
                cols = slice(h * HEAD_DIM, (h + 1) * HEAD_DIM)
                scores = lax.dot_general(
                    q_ref[:, cols],
                    k_ref[0:n, cols],
                    (((1,), (1,)), ((), ())),
                    preferred_element_type=jnp.float32,
                )
                scores = jnp.where(visible, scores, -1e30)
                top = jnp.max(scores, axis=1, keepdims=True)
                weights = jnp.exp(scores - top)
                total = jnp.maximum(jnp.sum(weights, axis=1, keepdims=True), 1.0)
                scale = jnp.where(live, 1.0 / total, 0.0)
                probs = (weights * scale).astype(jnp.bfloat16)
                o_ref[:, cols] = jnp.dot(
                    probs, v_ref[0:n, cols], preferred_element_type=jnp.float32
                ).astype(o_ref.dtype)


def attend(query, kv, segments):
    positions, width = query.shape
    block = Q_BLOCK
    position = jnp.arange(positions, dtype=jnp.int32)
    first = jnp.concatenate([jnp.ones((1,), bool), segments[1:] != segments[:-1]])
    lo = lax.cummax(jnp.where(first, position, 0), axis=0)
    hi = jnp.where(segments >= 0, position, -1)
    kernel = functools.partial(attention_kernel, block=block)
    return pl.pallas_call(
        kernel,
        grid=(positions // block,),
        in_specs=[
            pl.BlockSpec((block, width), lambda i: (i, 0)),
            pl.BlockSpec((positions, width), lambda i: (0, 0)),
            pl.BlockSpec((positions, width), lambda i: (0, 1)),
            pl.BlockSpec((block, 1), lambda i: (i, 0)),
            pl.BlockSpec((block, 1), lambda i: (i, 0)),
        ],
        out_specs=pl.BlockSpec((block, width), lambda i: (i, 0)),
        out_shape=jax.ShapeDtypeStruct((positions, width), query.dtype),
    )(query, kv, kv, lo.reshape(positions, 1), hi.reshape(positions, 1))


def send_pages(kv, page_table):
    pages = page_table.shape[0]
    positions, width = kv.shape
    page_rows = positions // pages
    heads = width // (2 * HEAD_DIM)
    paged = kv.reshape(pages, page_rows, width)
    target = page_table // pages
    local_slot = page_table % pages
    order = jnp.argsort(target, stable=True)
    slots = lax.all_to_all(local_slot[order], "req", split_axis=0, concat_axis=0, tiled=True)
    inverse = jnp.argsort(slots)
    moved = lax.all_to_all(paged[order], "req", split_axis=0, concat_axis=0, tiled=True)
    return place_pages(moved, inverse, heads)


def place_kernel(inverse_ref, moved_ref, out_ref):
    kinds, heads = out_ref.shape[0], out_ref.shape[1]

    def body(slot, carry):
        page = moved_ref[inverse_ref[slot]]
        for k in range(kinds):
            for h in range(heads):
                lo = (k * heads + h) * HEAD_DIM
                out_ref[k, h, slot] = page[:, lo : lo + HEAD_DIM]
        return carry

    lax.fori_loop(0, out_ref.shape[2], body, 0)


def place_pages(moved, inverse, heads):
    pages, page_rows, _ = moved.shape
    shape = (2, heads, pages, page_rows, HEAD_DIM)
    return pl.pallas_call(
        place_kernel,
        grid_spec=pltpu.PrefetchScalarGridSpec(
            num_scalar_prefetch=1,
            grid=(1,),
            in_specs=[pl.BlockSpec(moved.shape, lambda i, inv: (0, 0, 0))],
            out_specs=pl.BlockSpec(shape, lambda i, inv: (0, 0, 0, 0, 0)),
        ),
        out_shape=jax.ShapeDtypeStruct(shape, moved.dtype),
    )(inverse.astype(jnp.int32), moved)


def project_all(normed_local, w_query, w_key, w_value, qkv_bias, live):
    w_kv = jnp.concatenate([w_key, w_value], axis=1)
    normed = lax.all_gather(normed_local, "tp", axis=0, tiled=True)
    bias_kv = jnp.concatenate([qkv_bias[1], qkv_bias[2]])
    kv = jnp.where(
        live[:, None], jnp.dot(normed, w_kv, preferred_element_type=jnp.float32) + bias_kv, 0.0
    ).astype(jnp.bfloat16)
    query = (
        (jnp.dot(normed, w_query, preferred_element_type=jnp.float32) + qkv_bias[0])
        * HEAD_DIM ** (-0.5)
    ).astype(jnp.bfloat16)
    return (query, kv)


def on_device(
    hidden_in, ln_gain, ln_bias, w_query, w_key, w_value, qkv_bias, segment_ids, page_table
):
    query, kv = project_all(
        layer_norm(hidden_in, ln_gain, ln_bias),
        w_query,
        w_key,
        w_value,
        qkv_bias,
        segment_ids >= 0,
    )
    context = attend(query, kv, segment_ids)
    kv_cache = send_pages(kv, page_table)
    return (context, kv_cache)


def solution(mesh):
    return jax.shard_map(
        on_device,
        mesh=mesh,
        in_specs=(
            P(("req", "tp"), None),
            P(),
            P(),
            P(None, "tp"),
            P(None, "tp"),
            P(None, "tp"),
            P(None, "tp"),
            P("req"),
            P("req"),
        ),
        out_specs=(P("req", "tp"), P(None, "tp", "req", None, None)),
        check_vma=False,
    )
```

```python
import functools

import jax
import jax.numpy as jnp
from jax import lax
from jax.experimental import pallas as pl
from jax.experimental.pallas import tpu as pltpu
from jax.sharding import PartitionSpec as P

HEAD_DIM = 128
Q_BLOCK = 512


def layer_norm(rows, gain, shift):
    values = rows.astype(jnp.float32)
    center = values - jnp.mean(values, axis=1, keepdims=True)
    spread = jnp.mean(center * center, axis=1, keepdims=True)
    return (center * lax.rsqrt(spread + 1e-05) * gain + shift).astype(jnp.bfloat16)


def attention_kernel(q_ref, k_ref, v_ref, lo_ref, hi_ref, o_ref, *, block):
    qb = pl.program_id(0)
    for b in range(k_ref.shape[0] // block):

        @pl.when(qb == b)
        def _():
            n = (b + 1) * block
            col = lax.broadcasted_iota(jnp.int32, (block, n), 1)
            lo = lo_ref[...]
            hi = hi_ref[...]
            visible = (col >= lo) & (col <= hi)
            live = hi >= 0
            for h in range(q_ref.shape[1] // HEAD_DIM):
                cols = slice(h * HEAD_DIM, (h + 1) * HEAD_DIM)
                scores = lax.dot_general(
                    q_ref[:, cols],
                    k_ref[0:n, cols],
                    (((1,), (1,)), ((), ())),
                    preferred_element_type=jnp.float32,
                )
                scores = jnp.where(visible, scores, -1e30)
                top = jnp.max(scores, axis=1, keepdims=True)
                weights = jnp.exp(scores - top)
                total = jnp.maximum(jnp.sum(weights, axis=1, keepdims=True), 1.0)
                scale = jnp.where(live, 1.0 / total, 0.0)
                probs = (weights * scale).astype(jnp.bfloat16)
                o_ref[:, cols] = jnp.dot(
                    probs, v_ref[0:n, cols], preferred_element_type=jnp.float32
                ).astype(o_ref.dtype)


def attend(query, kv, segments):
    positions, width = query.shape
    block = Q_BLOCK
    position = jnp.arange(positions, dtype=jnp.int32)
    first = jnp.concatenate([jnp.ones((1,), bool), segments[1:] != segments[:-1]])
    lo = lax.cummax(jnp.where(first, position, 0), axis=0).reshape(positions, 1)
    hi = jnp.where(segments >= 0, position, -1).reshape(positions, 1)
    kernel = functools.partial(attention_kernel, block=block)
    return pl.pallas_call(
        kernel,
        grid=(positions // block,),
        in_specs=[
            pl.BlockSpec((block, width), lambda i: (i, 0)),
            pl.BlockSpec((positions, width), lambda i: (0, 0)),
            pl.BlockSpec((positions, width), lambda i: (0, 1)),
            pl.BlockSpec((block, 1), lambda i: (i, 0)),
            pl.BlockSpec((block, 1), lambda i: (i, 0)),
        ],
        out_specs=pl.BlockSpec((block, width), lambda i: (i, 0)),
        out_shape=jax.ShapeDtypeStruct((positions, width), query.dtype),
    )(query, kv, kv, lo, hi)


def send_pages(kv, page_table):
    pages = page_table.shape[0]
    positions, width = kv.shape
    page_rows = positions // pages
    heads = width // (2 * HEAD_DIM)
    paged = kv.reshape(pages, page_rows, width)
    target = page_table // pages
    local_slot = page_table % pages
    order = jnp.argsort(target, stable=True)
    slots = lax.all_to_all(local_slot[order], "req", split_axis=0, concat_axis=0, tiled=True)
    inverse = jnp.argsort(slots)
    moved = lax.all_to_all(paged[order], "req", split_axis=0, concat_axis=0, tiled=True)
    return place_pages(moved, inverse, heads)


def place_kernel(inverse_ref, moved_ref, out_ref):
    kinds, heads = out_ref.shape[0], out_ref.shape[1]

    def body(slot, carry):
        page = moved_ref[inverse_ref[slot]]
        for k in range(kinds):
            for h in range(heads):
                lo = (k * heads + h) * HEAD_DIM
                out_ref[k, h, slot] = page[:, lo : lo + HEAD_DIM]
        return carry

    lax.fori_loop(0, out_ref.shape[2], body, 0)


def place_pages(moved, inverse, heads):
    pages, page_rows, _ = moved.shape
    shape = (2, heads, pages, page_rows, HEAD_DIM)
    return pl.pallas_call(
        place_kernel,
        grid_spec=pltpu.PrefetchScalarGridSpec(
            num_scalar_prefetch=1,
            grid=(1,),
            in_specs=[pl.BlockSpec(moved.shape, lambda i, inv: (0, 0, 0))],
            out_specs=pl.BlockSpec(shape, lambda i, inv: (0, 0, 0, 0, 0)),
        ),
        out_shape=jax.ShapeDtypeStruct(shape, moved.dtype),
    )(inverse.astype(jnp.int32), moved)


def project_all(normed_local, w_query, w_key, w_value, qkv_bias, live):
    w_kv = jnp.concatenate([w_key, w_value], axis=1)
    normed = lax.all_gather(normed_local, "tp", axis=0, tiled=True)
    bias_kv = jnp.concatenate([qkv_bias[1], qkv_bias[2]])
    kv = jnp.where(
        live[:, None], jnp.dot(normed, w_kv, preferred_element_type=jnp.float32) + bias_kv, 0.0
    ).astype(jnp.bfloat16)
    query = (
        (jnp.dot(normed, w_query, preferred_element_type=jnp.float32) + qkv_bias[0])
        * HEAD_DIM ** (-0.5)
    ).astype(jnp.bfloat16)
    return (query, kv)


def on_device(
    hidden_in, ln_gain, ln_bias, w_query, w_key, w_value, qkv_bias, segment_ids, page_table
):
    query, kv = project_all(
        layer_norm(hidden_in, ln_gain, ln_bias),
        w_query,
        w_key,
        w_value,
        qkv_bias,
        segment_ids >= 0,
    )
    context = attend(query, kv, segment_ids)
    kv_cache = send_pages(kv, page_table)
    return (context, kv_cache)


def solution(mesh):
    return jax.shard_map(
        on_device,
        mesh=mesh,
        in_specs=(
            P(("req", "tp"), None),
            P(),
            P(),
            P(None, "tp"),
            P(None, "tp"),
            P(None, "tp"),
            P(None, "tp"),
            P("req"),
            P("req"),
        ),
        out_specs=(P("req", "tp"), P(None, "tp", "req", None, None)),
        check_vma=False,
    )
```

```python
import functools

import jax
import jax.numpy as jnp
from jax import lax
from jax.experimental import pallas as pl
from jax.experimental.pallas import tpu as pltpu
from jax.sharding import PartitionSpec as P

HEAD_DIM = 128
Q_BLOCK = 512
LN_BLOCK = 64


def layer_norm_kernel(x_ref, g_ref, b_ref, o_ref):
    values = x_ref[...].astype(jnp.float32)
    center = values - jnp.mean(values, axis=1, keepdims=True)
    spread = jnp.mean(center * center, axis=1, keepdims=True)
    o_ref[...] = (center * lax.rsqrt(spread + 1e-05) * g_ref[...] + b_ref[...]).astype(o_ref.dtype)


def layer_norm(rows, gain, shift):
    count, width = rows.shape
    block = LN_BLOCK
    return pl.pallas_call(
        layer_norm_kernel,
        grid=(count // block,),
        in_specs=[
            pl.BlockSpec((block, width), lambda i: (i, 0)),
            pl.BlockSpec((1, width), lambda i: (0, 0)),
            pl.BlockSpec((1, width), lambda i: (0, 0)),
        ],
        out_specs=pl.BlockSpec((block, width), lambda i: (i, 0)),
        out_shape=jax.ShapeDtypeStruct((count, width), jnp.bfloat16),
    )(rows, gain.reshape(1, width), shift.reshape(1, width))


def attention_kernel(q_ref, k_ref, v_ref, lo_ref, hi_ref, o_ref, *, block):
    qb = pl.program_id(0)
    for b in range(k_ref.shape[0] // block):

        @pl.when(qb == b)
        def _():
            n = (b + 1) * block
            col = lax.broadcasted_iota(jnp.int32, (block, n), 1)
            lo = lo_ref[...]
            hi = hi_ref[...]
            visible = (col >= lo) & (col <= hi)
            live = hi >= 0
            for h in range(q_ref.shape[1] // HEAD_DIM):
                cols = slice(h * HEAD_DIM, (h + 1) * HEAD_DIM)
                scores = lax.dot_general(
                    q_ref[:, cols],
                    k_ref[0:n, cols],
                    (((1,), (1,)), ((), ())),
                    preferred_element_type=jnp.float32,
                )
                scores = jnp.where(visible, scores, -1e30)
                top = jnp.max(scores, axis=1, keepdims=True)
                weights = jnp.exp(scores - top)
                total = jnp.maximum(jnp.sum(weights, axis=1, keepdims=True), 1.0)
                scale = jnp.where(live, 1.0 / total, 0.0)
                probs = (weights * scale).astype(jnp.bfloat16)
                o_ref[:, cols] = jnp.dot(
                    probs, v_ref[0:n, cols], preferred_element_type=jnp.float32
                ).astype(o_ref.dtype)


def attend(query, kv, segments):
    positions, width = query.shape
    block = Q_BLOCK
    position = jnp.arange(positions, dtype=jnp.int32)
    first = jnp.concatenate([jnp.ones((1,), bool), segments[1:] != segments[:-1]])
    lo = lax.cummax(jnp.where(first, position, 0), axis=0).reshape(positions, 1)
    hi = jnp.where(segments >= 0, position, -1).reshape(positions, 1)
    kernel = functools.partial(attention_kernel, block=block)
    return pl.pallas_call(
        kernel,
        grid=(positions // block,),
        in_specs=[
            pl.BlockSpec((block, width), lambda i: (i, 0)),
            pl.BlockSpec((positions, width), lambda i: (0, 0)),
            pl.BlockSpec((positions, width), lambda i: (0, 1)),
            pl.BlockSpec((block, 1), lambda i: (i, 0)),
            pl.BlockSpec((block, 1), lambda i: (i, 0)),
        ],
        out_specs=pl.BlockSpec((block, width), lambda i: (i, 0)),
        out_shape=jax.ShapeDtypeStruct((positions, width), query.dtype),
    )(query, kv, kv, lo, hi)


def send_pages(kv, page_table):
    pages = page_table.shape[0]
    positions, width = kv.shape
    page_rows = positions // pages
    heads = width // (2 * HEAD_DIM)
    paged = kv.reshape(pages, page_rows, width)
    target = page_table // pages
    local_slot = page_table % pages
    order = jnp.argsort(target, stable=True)
    slots = lax.all_to_all(local_slot[order], "req", split_axis=0, concat_axis=0, tiled=True)
    inverse = jnp.argsort(slots)
    moved = lax.all_to_all(paged[order], "req", split_axis=0, concat_axis=0, tiled=True)
    return place_pages(moved, inverse, heads)


def place_kernel(inverse_ref, moved_ref, out_ref):
    kinds, heads = out_ref.shape[0], out_ref.shape[1]

    def body(slot, carry):
        page = moved_ref[inverse_ref[slot]]
        for k in range(kinds):
            for h in range(heads):
                lo = (k * heads + h) * HEAD_DIM
                out_ref[k, h, slot] = page[:, lo : lo + HEAD_DIM]
        return carry

    lax.fori_loop(0, out_ref.shape[2], body, 0)


def place_pages(moved, inverse, heads):
    pages, page_rows, _ = moved.shape
    shape = (2, heads, pages, page_rows, HEAD_DIM)
    return pl.pallas_call(
        place_kernel,
        grid_spec=pltpu.PrefetchScalarGridSpec(
            num_scalar_prefetch=1,
            grid=(1,),
            in_specs=[pl.BlockSpec(moved.shape, lambda i, inv: (0, 0, 0))],
            out_specs=pl.BlockSpec(shape, lambda i, inv: (0, 0, 0, 0, 0)),
        ),
        out_shape=jax.ShapeDtypeStruct(shape, moved.dtype),
    )(inverse.astype(jnp.int32), moved)


def project_all(normed_local, w_query, w_key, w_value, qkv_bias, live):
    w_kv = jnp.concatenate([w_key, w_value], axis=1)
    normed = lax.all_gather(normed_local, "tp", axis=0, tiled=True)
    bias_kv = jnp.concatenate([qkv_bias[1], qkv_bias[2]])
    kv = jnp.where(
        live[:, None], jnp.dot(normed, w_kv, preferred_element_type=jnp.float32) + bias_kv, 0.0
    ).astype(jnp.bfloat16)
    query = (
        (jnp.dot(normed, w_query, preferred_element_type=jnp.float32) + qkv_bias[0])
        * HEAD_DIM ** (-0.5)
    ).astype(jnp.bfloat16)
    return (query, kv)


def on_device(
    hidden_in, ln_gain, ln_bias, w_query, w_key, w_value, qkv_bias, segment_ids, page_table
):
    query, kv = project_all(
        layer_norm(hidden_in, ln_gain, ln_bias),
        w_query,
        w_key,
        w_value,
        qkv_bias,
        segment_ids >= 0,
    )
    context = attend(query, kv, segment_ids)
    kv_cache = send_pages(kv, page_table)
    return (context, kv_cache)


def solution(mesh):
    return jax.shard_map(
        on_device,
        mesh=mesh,
        in_specs=(
            P(("req", "tp"), None),
            P(),
            P(),
            P(None, "tp"),
            P(None, "tp"),
            P(None, "tp"),
            P(None, "tp"),
            P("req"),
            P("req"),
        ),
        out_specs=(P("req", "tp"), P(None, "tp", "req", None, None)),
        check_vma=False,
    )
```
